32 devices in a mesh: dp: 32 (over z, y, x, core).
Axes of the slice: x: 2, y: 2, z: 4, core: 2. Of those that a mesh axis runs over, the one named last changes fastest.
Arguments:
- block_input: bfloat16 [4096, 960], P('dp'), may hold values from -6 to 6
- out_cotangent: bfloat16 [4096, 960], P('dp'), may hold values from -6 to 6
- w_query: bfloat16 [921600], P('dp'), may hold values from -0.1875 to 0.1875
- w_key: bfloat16 [307200], P('dp'), may hold values from -0.1875 to 0.1875
- w_value: bfloat16 [307200], P('dp'), may hold values from -0.1875 to 0.1875
- w_out: bfloat16 [921600], P('dp'), may hold values from -0.5 to 0.5
- w_gate: bfloat16 [2457600], P('dp'), may hold values from -0.1875 to 0.1875
- w_up: bfloat16 [2457600], P('dp'), may hold values from -0.1875 to 0.1875
- w_down: bfloat16 [2457600], P('dp'), may hold values from -0.125 to 0.125
- gain_attention: float32 [960], replicated, may hold values from 0.1 to 1.9
- gain_mlp: float32 [960], replicated, may hold values from 0.1 to 1.9
- seq_lengths: int32 [128], replicated, may hold values from 1 to 125, as said below
- seq_device: int32 [128], replicated, may hold values from 0 to 31, as said below
Outputs:
- block_out: bfloat16 [4096, 960], P('dp')
- grad_input: bfloat16 [4096, 960], P('dp')
- grad_query: float32 [921600], P('dp')
- grad_key: float32 [307200], P('dp')
- grad_value: float32 [307200], P('dp')
- grad_out: float32 [921600], P('dp')
- grad_gate: float32 [2457600], P('dp')
- grad_up: float32 [2457600], P('dp')
- grad_down: float32 [2457600], P('dp')
- grad_gain_attention: float32 [960], replicated
- grad_gain_mlp: float32 [960], replicated
The draws below stay inside these ranges and needn't reach their ends.
Inputs may be any that keep to these rules, and one draw needn't show every extreme that they name: `seq_lengths`: every sequence has at least one token; the lengths of the sequences dealt to one device sum to at most 128, and to exactly 128 on at least one device, where one sequence takes 128 - 3 slots. `seq_device`: every device is dealt exactly 4 sequences.
All inputs are finite; a program needn't handle non-finite values.
Results may differ from the reference program's by a relative error of at most 0.012.
Values may be sent and summed in bfloat16 or wider, within the bound.
No kernel may reach another device: no remote copies, remote signals or barrier semaphores. Data moves between devices by JAX's collectives and lax.ppermute only.
A program may use at most 192 MiB of HBM per device.

```python
import math
import jax
import jax.numpy as jnp
from jax import lax

D = 960
HEADS = 15
KV_HEADS = 5
HEAD_DIM = 64
FF = 2560
TOK_DEV = 128
SEQ_DEV = 4
SEQS = 128
TOKENS = 4096
N_DP = 32


def deal_sequences(key):
    base = jax.random.fold_in(key, 17)
    first_key, second_key, third_key, fourth_key = jax.random.split(base, 4)
    device_count = SEQS // SEQ_DEV
    order = jax.random.permutation(first_key, SEQS).astype(jnp.int32)
    owners = (jnp.arange(SEQS, dtype=jnp.int32) // SEQ_DEV).astype(jnp.int32)
    seq_device = jnp.zeros((SEQS,), jnp.int32).at[order].set(owners)
    levels = jax.random.randint(second_key, (device_count,), 0, 65).astype(jnp.int32)
    lowest = TOK_DEV // 8
    budgets = lowest + levels * levels * (TOK_DEV - lowest) // 4096
    chosen = jax.random.randint(third_key, (), 0, device_count).astype(jnp.int32)
    is_chosen = jnp.arange(device_count, dtype=jnp.int32) == chosen
    budgets = jnp.where(is_chosen, TOK_DEV, budgets).astype(jnp.int32)
    spare = budgets - SEQ_DEV
    cuts = jax.random.randint(fourth_key, (device_count, SEQ_DEV - 1), 0, spare[:, None] + 1).astype(jnp.int32)
    cuts = jnp.where(is_chosen[:, None], 0, cuts).astype(jnp.int32)
    cuts = jnp.sort(cuts, axis=-1)
    bounds = jnp.concatenate([jnp.zeros((device_count, 1), jnp.int32), cuts, spare[:, None]], axis=-1)
    parts = (bounds[:, 1:] - bounds[:, :-1] + 1).astype(jnp.int32)
    seq_lengths = jnp.zeros((SEQS,), jnp.int32).at[order].set(parts.reshape(-1))
    return (seq_lengths, seq_device)


def draw_seq_lengths(key, part):
    return deal_sequences(key)[0]


def draw_seq_device(key, part):
    return deal_sequences(key)[1]


def steps_of(own_key, dims, cuts, smallest, high):
    loudness, own = 1.0, jax.random.fold_in(own_key, 6)
    for dim, blocks in cuts:
        draws = jnp.exp(jax.random.uniform(jax.random.fold_in(own, dim), (blocks,), jnp.float32, smallest / len(cuts), high / len(cuts)))
        loudness = loudness * jnp.repeat(draws, dims[dim] // blocks).reshape([-1 if axis == dim else 1 for axis in range(len(dims))])
    return loudness


def noise(rng, dims, scale, reach, cuts=(), held_as=jnp.bfloat16):
    result = scale * jax.random.normal(rng, dims, jnp.float32)
    if cuts:
        result = result * steps_of(rng, dims, cuts, -0.22, 0.18)
    return jnp.clip(result, -reach, reach).astype(held_as)


def setup_inputs(seed: int = 0) -> dict:
    arg_keys = jax.random.split(jax.random.key(seed), 14)
    block_input = noise(arg_keys[0], (TOKENS, D), 1.0, 6.0, ((0, 32),))
    out_cotangent = noise(arg_keys[1], (TOKENS, D), 1.0, 6.0, ((0, 32),))
    w_query = noise(arg_keys[2], (D * D,), D ** -0.5, 0.1875, ((0, 32),))
    w_key = noise(arg_keys[3], (D * KV_HEADS * HEAD_DIM,), D ** -0.5, 0.1875, ((0, 32),))
    w_value = noise(arg_keys[4], (D * KV_HEADS * HEAD_DIM,), D ** -0.5, 0.1875, ((0, 32),))
    w_out = noise(arg_keys[5], (D * D,), (D // 8) ** -0.5, 0.5, ((0, 32),))
    w_gate = noise(arg_keys[6], (D * FF,), D ** -0.5, 0.1875, ((0, 32),))
    w_up = noise(arg_keys[7], (D * FF,), D ** -0.5, 0.1875, ((0, 32),))
    w_down = noise(arg_keys[8], (FF * D,), FF ** -0.5, 0.125, ((0, 32),))
    gain_attention = jnp.clip(1.0 + 0.18 * jax.random.normal(arg_keys[9], (D,), jnp.float32), 0.1, 1.9)
    gain_mlp = jnp.clip(1.0 + 0.18 * jax.random.normal(arg_keys[10], (D,), jnp.float32), 0.1, 1.9)
    seq_lengths = draw_seq_lengths(jax.random.fold_in(arg_keys[13], 71), 0)
    seq_device = draw_seq_device(jax.random.fold_in(arg_keys[13], 71), 0)
    return {"block_input": block_input, "out_cotangent": out_cotangent, "w_query": w_query, "w_key": w_key, "w_value": w_value, "w_out": w_out, "w_gate": w_gate, "w_up": w_up, "w_down": w_down, "gain_attention": gain_attention, "gain_mlp": gain_mlp, "seq_lengths": seq_lengths, "seq_device": seq_device}


def product(pattern, left, right):
    return jnp.einsum(pattern, left.astype(jnp.float32), right.astype(jnp.float32))

def slot_layout(seq_lengths, seq_device, my_index, tok_rows):
    is_mine = seq_device == my_index
    my_lengths = jnp.where(is_mine, seq_lengths, 0).astype(jnp.int32)
    seq_starts = (jnp.cumsum(my_lengths) - my_lengths).astype(jnp.int32)
    slot_ids = jnp.arange(tok_rows, dtype=jnp.int32)
    inside_seq = is_mine[None, :] & (slot_ids[:, None] >= seq_starts[None, :]) & (slot_ids[:, None] < (seq_starts + my_lengths)[None, :])
    seq_ids = jnp.arange(seq_lengths.shape[0], dtype=jnp.int32)
    live_slot = jnp.any(inside_seq, axis=1)
    segment = jnp.where(live_slot, lax.optimization_barrier(jnp.sum(jnp.where(inside_seq, seq_ids[None, :], 0), axis=1)).astype(jnp.int32), -1 - slot_ids)
    position = lax.optimization_barrier(jnp.sum(jnp.where(inside_seq, slot_ids[:, None] - seq_starts[None, :], 0), axis=1)).astype(jnp.int32)
    return (live_slot, segment, position)

def rms_norm(values):
    inv_rms = lax.rsqrt(lax.optimization_barrier(jnp.mean(values * values, axis=-1, keepdims=True)) + 1e-05)
    return (values * inv_rms, inv_rms)

def rms_norm_back(grad_normed, normed, inv_rms, gain):
    scaled = grad_normed * gain
    grad_values = inv_rms * (scaled - normed * lax.optimization_barrier(jnp.mean(scaled * normed, axis=-1, keepdims=True)))
    return (lax.optimization_barrier(jnp.sum(grad_normed * normed, axis=0)), grad_values)

def rotary_tables(position, half_dim):
    inv_freq = jnp.exp(-jnp.arange(half_dim, dtype=jnp.float32) * (math.log(100000.0) / half_dim))
    angles = position.astype(jnp.float32)[:, None] * inv_freq[None, :]
    return (jnp.cos(angles)[:, None, :], jnp.sin(angles)[:, None, :])

def rotary(values, cos_table, sin_table):
    half_dim = values.shape[-1] // 2
    first_half = values[..., :half_dim]
    second_half = values[..., half_dim:]
    return jnp.concatenate([first_half * cos_table - second_half * sin_table, second_half * cos_table + first_half * sin_table], axis=-1)

def rotary_back(grads, cos_table, sin_table):
    half_dim = grads.shape[-1] // 2
    first_half = grads[..., :half_dim]
    second_half = grads[..., half_dim:]
    return jnp.concatenate([first_half * cos_table + second_half * sin_table, second_half * cos_table - first_half * sin_table], axis=-1)

def attention_mask(segment, tok_rows):
    slot_ids = jnp.arange(tok_rows, dtype=jnp.int32)
    return (segment[:, None] == segment[None, :]) & (slot_ids[None, :] <= slot_ids[:, None])

def masked_scores(query_rot, key_rot, key_mask):
    tok_rows = query_rot.shape[0]
    grouped = query_rot.reshape(tok_rows, KV_HEADS, HEADS // KV_HEADS, HEAD_DIM)
    logits = product('tkgd,skd->kgts', grouped, key_rot) * (1.0 / math.sqrt(HEAD_DIM))
    return (jnp.where(key_mask, logits, -1e+30), grouped)

def forward(block_input, attend_weights, feed_weights, gain_attention, gain_mlp, live_slot, segment, position):
    w_query, w_key, w_value, w_out = attend_weights
    w_gate, w_up, w_down = feed_weights
    tok_rows = block_input.shape[0]
    block_f32 = block_input.astype(jnp.float32)
    normed_one, inv_rms_one = rms_norm(block_f32)
    normed_in = (normed_one * gain_attention).astype(jnp.bfloat16)
    cos_table, sin_table = rotary_tables(position, HEAD_DIM // 2)
    query_f32 = product('td,de->te', normed_in, w_query).reshape(tok_rows, HEADS, HEAD_DIM)
    key_f32 = product('td,de->te', normed_in, w_key).reshape(tok_rows, KV_HEADS, HEAD_DIM)
    value_f32 = product('td,de->te', normed_in, w_value).reshape(tok_rows, KV_HEADS, HEAD_DIM)
    query_rot = rotary(query_f32, cos_table, sin_table).astype(jnp.bfloat16)
    key_rot = rotary(key_f32, cos_table, sin_table).astype(jnp.bfloat16)
    value_bf = value_f32.astype(jnp.bfloat16)
    key_mask = attention_mask(segment, tok_rows)
    logits, grouped = masked_scores(query_rot, key_rot, key_mask)
    row_max = lax.optimization_barrier(jnp.max(logits, axis=-1, keepdims=True))
    exp_terms = jnp.exp(logits - row_max)
    row_total = lax.optimization_barrier(jnp.sum(exp_terms, axis=-1, keepdims=True))
    log_total = row_max + jnp.log(row_total)
    prob_bf = (exp_terms / row_total).astype(jnp.bfloat16)
    attended = product('kgts,skd->tkgd', prob_bf, value_bf).reshape(tok_rows, HEADS * HEAD_DIM).astype(jnp.bfloat16)
    resid_mid = block_f32 + product('te,ed->td', attended, w_out)
    normed_two, inv_rms_two = rms_norm(resid_mid)
    normed_mid = (normed_two * gain_mlp).astype(jnp.bfloat16)
    gate_pre = product('td,df->tf', normed_mid, w_gate)
    up_proj = product('td,df->tf', normed_mid, w_up)
    hidden_act = (jax.nn.silu(gate_pre) * up_proj).astype(jnp.bfloat16)
    block_sum = resid_mid + product('tf,fd->td', hidden_act, w_down)
    block_out = jnp.where(live_slot[:, None], block_sum, 0.0).astype(jnp.bfloat16)
    saved = (normed_in, normed_one, inv_rms_one, query_rot, key_rot, value_bf, attended, log_total, key_mask, normed_two, inv_rms_two, normed_mid, gate_pre, up_proj, hidden_act, cos_table, sin_table)
    return (block_out, saved)

def backward_mlp(saved, out_cotangent, feed_weights, gain_mlp, live_slot):
    normed_two, inv_rms_two, normed_mid, gate_pre, up_proj, hidden_act = saved[9:15]
    w_gate, w_up, w_down = feed_weights
    grad_out_f32 = jnp.where(live_slot[:, None], out_cotangent.astype(jnp.float32), 0.0)
    grad_out_bf = grad_out_f32.astype(jnp.bfloat16)
    grad_down = product('tf,td->fd', hidden_act, grad_out_bf)
    grad_hidden = product('td,fd->tf', grad_out_bf, w_down)
    sigmoid_gate = jax.nn.sigmoid(gate_pre)
    grad_gate_pre = (grad_hidden * up_proj * sigmoid_gate * (1.0 + gate_pre * (1.0 - sigmoid_gate))).astype(jnp.bfloat16)
    grad_up_proj = (grad_hidden * gate_pre * sigmoid_gate).astype(jnp.bfloat16)
    grad_gate = product('td,tf->df', normed_mid, grad_gate_pre)
    grad_up = product('td,tf->df', normed_mid, grad_up_proj)
    grad_normed_mid = product('tf,df->td', grad_gate_pre, w_gate) + product('tf,df->td', grad_up_proj, w_up)
    gain_grad, grad_resid_norm = rms_norm_back(grad_normed_mid, normed_two, inv_rms_two, gain_mlp)
    return (grad_out_f32 + grad_resid_norm, (grad_gate, grad_up, grad_down), gain_grad)

def backward_attention(saved, grad_resid, attend_weights, gain_attention, live_slot):
    normed_in, normed_one, inv_rms_one, query_rot, key_rot, value_bf, attended, log_total, key_mask = saved[:9]
    cos_table, sin_table = saved[15:]
    w_query, w_key, w_value, w_out = attend_weights
    tok_rows = attended.shape[0]
    group_size = HEADS // KV_HEADS
    score_scale = 1.0 / math.sqrt(HEAD_DIM)
    grad_resid_bf = grad_resid.astype(jnp.bfloat16)
    grad_wout = product('te,td->ed', attended, grad_resid_bf)
    grad_attended = product('td,ed->te', grad_resid_bf, w_out).astype(jnp.bfloat16)
    grad_att_group = grad_attended.reshape(tok_rows, KV_HEADS, group_size, HEAD_DIM)
    att_group = attended.reshape(tok_rows, KV_HEADS, group_size, HEAD_DIM)
    logits, grouped = masked_scores(query_rot, key_rot, key_mask)
    probs = jnp.exp(logits - log_total)
    prob_bf = probs.astype(jnp.bfloat16)
    grad_value_f32 = product('kgts,tkgd->skd', prob_bf, grad_att_group)
    grad_probs = product('tkgd,skd->kgts', grad_att_group, value_bf)
    row_delta = lax.optimization_barrier(jnp.sum(grad_att_group.astype(jnp.float32) * att_group.astype(jnp.float32), axis=-1))
    row_delta = jnp.transpose(row_delta, (1, 2, 0))[..., None]
    grad_logits = (probs * (grad_probs - row_delta)).astype(jnp.bfloat16)
    grad_query_rot = product('kgts,skd->tkgd', grad_logits, key_rot).reshape(tok_rows, HEADS, HEAD_DIM) * score_scale
    grad_key_rot = product('kgts,tkgd->skd', grad_logits, grouped) * score_scale
    grad_query_bf = rotary_back(grad_query_rot, cos_table, sin_table).reshape(tok_rows, -1).astype(jnp.bfloat16)
    grad_key_bf = rotary_back(grad_key_rot, cos_table, sin_table).reshape(tok_rows, -1).astype(jnp.bfloat16)
    grad_value_bf = grad_value_f32.reshape(tok_rows, -1).astype(jnp.bfloat16)
    grad_wquery = product('td,te->de', normed_in, grad_query_bf)
    grad_wkey = product('td,te->de', normed_in, grad_key_bf)
    grad_wvalue = product('td,te->de', normed_in, grad_value_bf)
    grad_normed_in = product('te,de->td', grad_query_bf, w_query) + product('te,de->td', grad_key_bf, w_key) + product('te,de->td', grad_value_bf, w_value)
    gain_grad, grad_input_norm = rms_norm_back(grad_normed_in, normed_one, inv_rms_one, gain_attention)
    grad_input = jnp.where(live_slot[:, None], grad_resid + grad_input_norm, 0.0).astype(jnp.bfloat16)
    return (grad_input, (grad_wquery, grad_wkey, grad_wvalue, grad_wout), gain_grad)

def reference(block_input, out_cotangent, w_query, w_key, w_value, w_out, w_gate, w_up, w_down, gain_attention, gain_mlp, seq_lengths, seq_device):
    kv_width = KV_HEADS * HEAD_DIM
    attend_weights = (w_query.reshape(D, D), w_key.reshape(D, kv_width), w_value.reshape(D, kv_width), w_out.reshape(D, D))
    feed_weights = (w_gate.reshape(D, FF), w_up.reshape(D, FF), w_down.reshape(FF, D))
    inputs_dev = block_input.reshape(N_DP, TOK_DEV, D)
    cotangents_dev = out_cotangent.reshape(N_DP, TOK_DEV, D)

    def scan_step(totals, device_item):
        my_index, input_rows, cotangent_rows = device_item
        live_slot, segment, position = slot_layout(seq_lengths, seq_device, my_index, TOK_DEV)
        block_rows, saved = forward(input_rows, attend_weights, feed_weights, gain_attention, gain_mlp, live_slot, segment, position)
        grad_resid, feed_grads, gain_mlp_grad = backward_mlp(saved, cotangent_rows, feed_weights, gain_mlp, live_slot)
        grad_rows, attend_grads, gain_attention_grad = backward_attention(saved, grad_resid, attend_weights, gain_attention, live_slot)
        pieces = attend_grads + feed_grads + (gain_attention_grad, gain_mlp_grad)
        summed = tuple((total + piece for total, piece in zip(totals, pieces)))
        return (summed, (block_rows, grad_rows))
    zeros_init = (jnp.zeros((D, D), jnp.float32), jnp.zeros((D, kv_width), jnp.float32), jnp.zeros((D, kv_width), jnp.float32), jnp.zeros((D, D), jnp.float32), jnp.zeros((D, FF), jnp.float32), jnp.zeros((D, FF), jnp.float32), jnp.zeros((FF, D), jnp.float32), jnp.zeros((D,), jnp.float32), jnp.zeros((D,), jnp.float32))
    totals, (block_rows, grad_rows) = lax.scan(scan_step, zeros_init, (jnp.arange(N_DP, dtype=jnp.int32), inputs_dev, cotangents_dev))
    return (block_rows.reshape(-1, D), grad_rows.reshape(-1, D), totals[0].reshape(-1), totals[1].reshape(-1), totals[2].reshape(-1), totals[3].reshape(-1), totals[4].reshape(-1), totals[5].reshape(-1), totals[6].reshape(-1), totals[7], totals[8])
```

```python
import math

import jax
import jax.numpy as jnp
from jax import lax
from jax.sharding import PartitionSpec as P

HEADS = 15
KV_HEADS = 5
HEAD_DIM = 64
OWNERS = 32
CHIPS = 16
F32 = jnp.float32
BF16 = jnp.bfloat16


def product(pattern, left, right):
    return jnp.einsum(pattern, left, right, preferred_element_type=F32)


def matmul(left, right):
    return jnp.dot(left, right, preferred_element_type=F32)


def slot_layout(seq_lengths, seq_device, my_index, tok_rows):
    is_mine = seq_device == my_index
    my_lengths = jnp.where(is_mine, seq_lengths, 0)
    seq_starts = jnp.cumsum(my_lengths) - my_lengths
    slot_ids = jnp.arange(tok_rows, dtype=jnp.int32)
    inside_seq = (
        is_mine[None, :]
        & (slot_ids[:, None] >= seq_starts[None, :])
        & (slot_ids[:, None] < (seq_starts + my_lengths)[None, :])
    )
    seq_ids = jnp.arange(seq_lengths.shape[0], dtype=jnp.int32)
    live_slot = jnp.any(inside_seq, axis=1)
    segment = jnp.where(
        live_slot, jnp.sum(jnp.where(inside_seq, seq_ids[None, :], 0), axis=1), -1 - slot_ids
    )
    position = jnp.sum(jnp.where(inside_seq, slot_ids[:, None] - seq_starts[None, :], 0), axis=1)
    return (live_slot, segment, position)


def rms_norm(values):
    inv_rms = lax.rsqrt(jnp.mean(values * values, axis=-1, keepdims=True) + 1e-05)
    return (values * inv_rms, inv_rms)


def rms_norm_back(grad_normed, normed, inv_rms, gain):
    scaled = grad_normed * gain
    grad_values = inv_rms * (scaled - normed * jnp.mean(scaled * normed, axis=-1, keepdims=True))
    return (jnp.sum(grad_normed * normed, axis=0), grad_values)


def rotary_tables(position, half_dim):
    inv_freq = jnp.exp(-jnp.arange(half_dim, dtype=F32) * (math.log(100000.0) / half_dim))
    angles = position.astype(F32)[:, None] * inv_freq[None, :]
    return (jnp.cos(angles)[:, None, :], jnp.sin(angles)[:, None, :])


def rotary(values, cos_table, sin_table):
    half_dim = values.shape[-1] // 2
    first_half = values[..., :half_dim]
    second_half = values[..., half_dim:]
    return jnp.concatenate(
        [
            first_half * cos_table - second_half * sin_table,
            second_half * cos_table + first_half * sin_table,
        ],
        axis=-1,
    )


def attention_mask(segment, tok_rows):
    slot_ids = jnp.arange(tok_rows, dtype=jnp.int32)
    return (segment[:, None] == segment[None, :]) & (slot_ids[None, :] <= slot_ids[:, None])


def masked_scores(query_rot, key_rot, key_mask):
    tok_rows = query_rot.shape[0]
    grouped = query_rot.reshape(tok_rows, KV_HEADS, HEADS // KV_HEADS, HEAD_DIM)
    logits = product("tkgd,skd->kgts", grouped, key_rot) * (1.0 / math.sqrt(HEAD_DIM))
    return (jnp.where(key_mask, logits, -1e30), grouped)


def gray(index):
    return index ^ (index >> 1)


def hops(spread):
    def along(step):
        return [
            (owner * spread + rest, step(owner) * spread + rest)
            for owner in range(OWNERS)
            for rest in range(spread)
        ]

    def ring_step(owner):
        depth = owner // 8
        return gray((gray(depth) + 1) % 4) * 8 + owner % 8

    return {
        "c": along(lambda owner: owner ^ 1),
        "x": along(lambda owner: owner ^ 2),
        "y": along(lambda owner: owner ^ 4),
        "z": along(ring_step),
    }


def mover(routes):
    def move(values, axis):
        return lax.ppermute(values, "dp", routes[axis])

    return move


def relative_owner(me, order, position):
    owner = me
    for axis in reversed(order):
        if axis == "z":
            digit = position % 4
            position = position // 4
            depth = owner // 8
            owner = gray((gray(depth) + 4 - digit) % 4) * 8 + owner % 8
        else:
            digit = position % 2
            position = position // 2
            owner = owner ^ (digit << {"c": 0, "x": 1, "y": 2}[axis])
    return owner


def selector(me, order, width, rows, padded):
    slots = jnp.arange(OWNERS * padded, dtype=jnp.int32)
    inside = slots % padded
    source = relative_owner(me, order, slots // padded) * rows + inside
    source = jnp.where(inside < rows, source, -1)
    features = jnp.arange(width, dtype=jnp.int32)
    return (features[:, None] == source[None, :]).astype(BF16)


def unselect(values, selecting):
    high = lax.reduce_precision(values, 8, 7)
    low = values - high
    return product("tp,fp->tf", high.astype(BF16), selecting) + product(
        "tp,fp->tf", low.astype(BF16), selecting
    )


def rows_of(*pieces):
    return jnp.concatenate(pieces, axis=0)


def add(left, right):
    return left.astype(F32) + right.astype(F32)


def ring_gather(move, block):
    pieces = [block]
    for _ in range(3):
        pieces.append(move(pieces[-1], "z"))
    return pieces


def ring_scatter(move, pieces):
    total = pieces[1]
    for piece in (pieces[2], pieces[3], pieces[0]):
        total = add(piece, move(total.astype(BF16), "z"))
    return total


def swap_gather(move, block, axis):
    return rows_of(block, move(block, axis))


def swap_scatter(move, block, axis):
    half = block.shape[0] // 2
    return add(block[:half], move(block[half:].astype(BF16), axis))


def pad_to(values, rows, columns):
    return jnp.pad(values, ((0, rows - values.shape[0]), (0, columns - values.shape[1])))


def local(
    block_input,
    out_cotangent,
    w_query,
    w_key,
    w_value,
    w_out,
    w_gate,
    w_up,
    w_down,
    gain_attention,
    gain_mlp,
    seq_lengths,
    seq_device,
):
    width = gain_attention.shape[0]
    tok_rows = block_input.shape[0]
    spread = lax.axis_size("dp") // OWNERS
    my_index = lax.axis_index("dp")
    me = my_index // spread
    core = me % 2
    move = mover(hops(spread))
    groups = [[owner * spread + rest for rest in range(spread)] for owner in range(OWNERS)]

    def whole_shard(weight):
        if spread == 1:
            return weight
        return lax.all_gather(weight, "dp", axis=0, tiled=True, axis_index_groups=groups)

    def own_shard(grads):
        if spread == 1:
            return grads
        return lax.psum_scatter(
            grads, "dp", scatter_dimension=0, tiled=True, axis_index_groups=groups
        )

    rows = width // OWNERS
    padded = -(-rows // 16) * 16
    kv_width = KV_HEADS * HEAD_DIM
    qkv_width = width + 2 * kv_width
    qkv_cols = -(-qkv_width // 128) * 128
    out_cols = -(-width // 128) * 128

    shard_qkv = jnp.concatenate(
        [
            whole_shard(w_query).reshape(rows, width),
            whole_shard(w_key).reshape(rows, kv_width),
            whole_shard(w_value).reshape(rows, kv_width),
        ],
        axis=1,
    )
    shard_out = whole_shard(w_out).reshape(rows, width)
    shard_attend = jnp.concatenate(
        [pad_to(shard_qkv, padded, qkv_cols), pad_to(shard_out, padded, out_cols)], axis=1
    )
    shard_down = whole_shard(w_down).reshape(-1, width)
    hid_rows = shard_down.shape[0]
    hid_half = CHIPS * hid_rows

    def column_halves(weight):
        split = whole_shard(weight).reshape(rows, CHIPS, 2, hid_rows)
        pair = [pad_to(split[:, :, k].reshape(rows, hid_half), padded, hid_half) for k in range(2)]
        return (jnp.where(core == 0, pair[0], pair[1]), jnp.where(core == 0, pair[1], pair[0]))

    gate_mine, gate_other = column_halves(w_gate)
    up_mine, up_other = column_halves(w_up)

    attend_ring = ring_gather(move, shard_attend)
    qkv_rel = rows_of(*[piece[:, :qkv_cols] for piece in attend_ring])
    out_rel = rows_of(*[piece[:, qkv_cols:] for piece in attend_ring])
    qkv_rel = swap_gather(move, swap_gather(move, qkv_rel, "x"), "y")
    out_rel = swap_gather(move, swap_gather(move, out_rel, "y"), "x")
    qkv_rel = swap_gather(move, qkv_rel, "c")
    out_rel = swap_gather(move, out_rel, "c")
    sel_qkv = selector(me, "cyxz", width, rows, padded)
    sel_out = selector(me, "cxyz", width, rows, padded)

    swapped = move(rows_of(gate_other, up_other), "c")
    gate_block = rows_of(gate_mine, swapped[:padded])
    up_block = rows_of(up_mine, swapped[padded:])
    gate_rel = ring_gather(
        move, swap_gather(move, swap_gather(move, gate_block, "x"), "y")
    )
    up_ring = rows_of(*ring_gather(move, swap_gather(move, up_block, "y")))
    up_rel = [up_ring, move(up_ring, "x")]
    down_ring = swap_gather(move, rows_of(*ring_gather(move, shard_down)), "x")
    down_rel = rows_of(down_ring, move(down_ring, "y"))
    sel_gate = selector(me, "zyxc", width, rows, padded)
    sel_up = selector(me, "xzyc", width, rows, padded)

    stands = jnp.arange(CHIPS, dtype=jnp.int32)
    chip_of_stand = relative_owner(me, "yxz", stands) // 2
    stand_of_chip = jnp.sum(
        jnp.where(chip_of_stand[None, :] == stands[:, None], stands[None, :], 0), axis=1
    )
    w_down_half = jnp.take(
        down_rel.reshape(CHIPS, hid_rows, width), stand_of_chip, axis=0
    ).reshape(hid_half, width)

    live_slot, segment, position = slot_layout(seq_lengths, seq_device, my_index, tok_rows)
    live = live_slot[:, None]
    grad_out_f32 = jnp.where(live, out_cotangent.astype(F32), 0.0)
    grad_out_bf = grad_out_f32.astype(BF16)
    grad_out_pair = swap_gather(move, grad_out_bf, "c")
    block_f32 = block_input.astype(F32)
    normed_one, inv_rms_one = rms_norm(block_f32)
    normed_in = (normed_one * gain_attention).astype(BF16)
    cos_table, sin_table = rotary_tables(position, HEAD_DIM // 2)
    key_mask = attention_mask(segment, tok_rows)
    qkv = matmul(matmul(normed_in, sel_qkv).astype(BF16), qkv_rel)
    query_f32 = qkv[:, :width].reshape(tok_rows, HEADS, HEAD_DIM)
    key_f32 = qkv[:, width : width + kv_width].reshape(tok_rows, KV_HEADS, HEAD_DIM)
    value_bf = qkv[:, width + kv_width : qkv_width].reshape(tok_rows, KV_HEADS, HEAD_DIM).astype(BF16)
    query_rot = rotary(query_f32, cos_table, sin_table).astype(BF16)
    key_rot = rotary(key_f32, cos_table, sin_table).astype(BF16)
    logits, grouped = masked_scores(query_rot, key_rot, key_mask)
    row_max = jnp.max(logits, axis=-1, keepdims=True)
    exp_terms = jnp.exp(logits - row_max)
    row_total = jnp.sum(exp_terms, axis=-1, keepdims=True)
    probs = exp_terms / row_total
    prob_bf = probs.astype(BF16)
    attended = product("kgts,skd->tkgd", prob_bf, value_bf).reshape(tok_rows, width).astype(BF16)
    attended_rel = matmul(attended, sel_out).astype(BF16)
    resid_mid = block_f32 + matmul(attended_rel, out_rel)[:, :width]

    normed_two, inv_rms_two = rms_norm(resid_mid)
    normed_mid = (normed_two * gain_mlp).astype(BF16)
    normed_pair = swap_gather(move, normed_mid, "c")
    mid_gate = matmul(normed_pair, sel_gate).astype(BF16)
    mid_up = matmul(normed_pair, sel_up).astype(BF16)
    depth = gate_rel[0].shape[0]
    mid_gate_parts = [mid_gate[:, k * depth : (k + 1) * depth] for k in range(4)]
    breadth = up_rel[0].shape[0]
    mid_up_parts = [mid_up[:, k * breadth : (k + 1) * breadth] for k in range(2)]
    gate_pre = sum(matmul(a, b) for a, b in zip(mid_gate_parts, gate_rel))
    up_proj = sum(matmul(a, b) for a, b in zip(mid_up_parts, up_rel))
    sigmoid_gate = jax.nn.sigmoid(gate_pre)
    silu_gate = gate_pre * sigmoid_gate
    hidden_act = (silu_gate * up_proj).astype(BF16)

    grad_down = product("tf,td->fd", hidden_act, grad_out_pair).astype(BF16)
    grad_hidden = product("td,fd->tf", grad_out_pair, w_down_half)
    grad_gate_pre = (
        grad_hidden * up_proj * sigmoid_gate * (1.0 + gate_pre * (1.0 - sigmoid_gate))
    ).astype(BF16)
    grad_up_proj = (grad_hidden * silu_gate).astype(BF16)
    grad_gate = [
        product("tr,tc->rc", part, grad_gate_pre).astype(BF16) for part in mid_gate_parts
    ]
    grad_up = product("tr,tc->rc", mid_up, grad_up_proj).astype(BF16)

    grad_down = jnp.take(
        grad_down.reshape(CHIPS, hid_rows, width), chip_of_stand, axis=0
    ).reshape(hid_half, width)
    down_part = swap_scatter(move, swap_scatter(move, grad_down, "y"), "x").astype(BF16)
    down_shard = ring_scatter(
        move, [down_part[k * hid_rows : (k + 1) * hid_rows] for k in range(4)]
    )
    gate_part = ring_scatter(move, grad_gate)
    gate_part = swap_scatter(move, swap_scatter(move, gate_part, "y"), "x")
    up_part = swap_scatter(move, grad_up, "x").astype(BF16)
    up_part = ring_scatter(
        move, [up_part[k * 4 * padded : (k + 1) * 4 * padded] for k in range(4)]
    )
    up_part = swap_scatter(move, up_part, "y")
    crossed = move(rows_of(gate_part[padded:], up_part[padded:]), "c")

    def join_halves(mine, other):
        first = jnp.where(core == 0, mine, other)[:rows].reshape(rows, CHIPS, hid_rows)
        second = jnp.where(core == 0, other, mine)[:rows].reshape(rows, CHIPS, hid_rows)
        return jnp.stack([first, second], axis=2).reshape(-1)

    gate_shard = join_halves(gate_part[:padded], crossed[:padded])
    up_shard = join_halves(up_part[:padded], crossed[padded:])

    dn_gate = jnp.concatenate(
        [product("tf,df->td", grad_gate_pre, part) for part in gate_rel], axis=1
    )
    dn_up = jnp.concatenate([product("tf,df->td", grad_up_proj, part) for part in up_rel], axis=1)
    dn_pair = unselect(dn_gate, sel_gate) + unselect(dn_up, sel_up)
    grad_normed_mid = dn_pair[:tok_rows] + move(dn_pair[tok_rows:], "c")
    gain_mlp_grad, grad_resid_norm = rms_norm_back(
        grad_normed_mid, normed_two, inv_rms_two, gain_mlp
    )
    grad_resid = grad_out_f32 + grad_resid_norm

    score_scale = 1.0 / math.sqrt(HEAD_DIM)
    grad_resid_bf = grad_resid.astype(BF16)
    grad_att_rel = product("td,ed->te", grad_resid_bf, out_rel[:, :width]).astype(BF16)
    grad_attended = product("tp,ep->te", grad_att_rel, sel_out).astype(BF16)
    att_shape = (tok_rows, KV_HEADS, HEADS // KV_HEADS, HEAD_DIM)
    grad_att_group = grad_attended.reshape(att_shape)
    att_group = attended.reshape(att_shape)
    grad_value_f32 = product("kgts,tkgd->skd", prob_bf, grad_att_group)
    grad_probs = product("tkgd,skd->kgts", grad_att_group, value_bf)
    row_delta = jnp.sum(grad_att_group.astype(F32) * att_group.astype(F32), axis=-1)
    row_delta = jnp.transpose(row_delta, (1, 2, 0))[..., None]
    grad_logits = (probs * (grad_probs - row_delta)).astype(BF16)
    grad_query_rot = (
        product("kgts,skd->tkgd", grad_logits, key_rot).reshape(tok_rows, HEADS, HEAD_DIM)
        * score_scale
    )
    grad_key_rot = product("kgts,tkgd->skd", grad_logits, grouped) * score_scale
    grad_qkv = jnp.concatenate(
        [
            rotary(grad_query_rot, cos_table, -sin_table).reshape(tok_rows, -1).astype(BF16),
            rotary(grad_key_rot, cos_table, -sin_table).reshape(tok_rows, -1).astype(BF16),
            grad_value_f32.reshape(tok_rows, -1).astype(BF16),
            jnp.zeros((tok_rows, qkv_cols - qkv_width), BF16),
        ],
        axis=1,
    )

    normed_both = swap_gather(move, normed_in, "c")
    attended_both = swap_gather(move, attended, "c")
    resid_both = swap_gather(move, grad_resid_bf, "c")
    qkv_both = swap_gather(move, grad_qkv, "c")
    side = OWNERS // 2 * padded
    left_qkv = matmul(normed_both, sel_qkv[:, :side]).astype(BF16)
    left_out = matmul(attended_both, sel_out[:, :side]).astype(BF16)
    grad_out_w = product("tr,tc->rc", left_out, pad_to(resid_both, 2 * tok_rows, out_cols))
    grad_out_w = swap_scatter(move, swap_scatter(move, grad_out_w.astype(BF16), "x"), "y")
    grad_qkv_w = product("tr,tc->rc", left_qkv, qkv_both)
    grad_qkv_w = swap_scatter(move, swap_scatter(move, grad_qkv_w.astype(BF16), "y"), "x")
    attend_part = jnp.concatenate([grad_qkv_w, grad_out_w], axis=1).astype(BF16)
    attend_shard = ring_scatter(
        move, [attend_part[k * padded : (k + 1) * padded] for k in range(4)]
    )[:rows]

    grad_normed_in = unselect(product("te,de->td", grad_qkv, qkv_rel), sel_qkv)
    gain_attention_grad, grad_input_norm = rms_norm_back(
        grad_normed_in, normed_one, inv_rms_one, gain_attention
    )
    grad_input = jnp.where(live, grad_resid + grad_input_norm, 0.0).astype(BF16)

    out_pair = matmul(hidden_act, w_down_half)
    block_sum = resid_mid + out_pair[:tok_rows] + move(out_pair[tok_rows:], "c")
    block_out = jnp.where(live, block_sum, 0.0).astype(BF16)

    gains = jnp.stack([gain_attention_grad, gain_mlp_grad])
    for axis in "cxy":
        gains = gains + move(gains, axis)
    gains = sum(ring_gather(move, gains))
    if spread > 1:
        gains = lax.psum(gains, "dp", axis_index_groups=[
            [owner * spread + rest for rest in range(spread)] for owner in range(OWNERS)
        ])

    return (
        block_out,
        grad_input,
        own_shard(attend_shard[:, :width].reshape(-1)),
        own_shard(attend_shard[:, width : width + kv_width].reshape(-1)),
        own_shard(attend_shard[:, width + kv_width : qkv_width].reshape(-1)),
        own_shard(attend_shard[:, qkv_cols : qkv_cols + width].reshape(-1)),
        own_shard(gate_shard),
        own_shard(up_shard),
        own_shard(down_shard.reshape(-1)),
        gains[0],
        gains[1],
    )


def solution(mesh):
    rows, flat, whole = P("dp", None), P("dp"), P()
    in_specs = (rows, rows) + (flat,) * 7 + (whole,) * 4
    out_specs = (rows, rows) + (flat,) * 7 + (whole,) * 2
    return jax.shard_map(local, mesh=mesh, in_specs=in_specs, out_specs=out_specs, check_vma=False)
```
